32 devices in a mesh: leaf: 8 (over z, core), sub: 4 (over y, x).
Axes of the slice: x: 2, y: 2, z: 4, core: 2. Of those that a mesh axis runs over, the one named last changes fastest.
Arguments:
- leaf_maps: float32 [32, 256, 1024], P('leaf', 'sub'), may hold values from -8 to 28, as said below
- order_one: int32 [8, 4], replicated, may hold values from 0 to 3, each once within a row
- order_two: int32 [4, 6], replicated, may hold values from 0 to 5, each once within a row
- top_data: float32 [16, 256, 256], P('leaf', 'sub'), may hold values from -6 to 6
Outputs:
- top_map: float32 [16, 256, 2048], P('leaf', 'sub')
- leaf_data: float32 [32, 256, 256], P('leaf', 'sub')
The draws below stay inside these ranges and needn't reach their ends.
Inputs may be any that keep to these rules, and one draw needn't show every extreme that they name: Each leaf's block of 1024 rows of leaf_maps, read as a 1024 by 1024 matrix, is symmetric and positive definite.
All inputs are finite; a program needn't handle non-finite values. Where the reference program divides by a largest or mean magnitude, that divisor is 1e-20 or more.
Results may differ from the reference program's by a relative error of at most 0.0001.
Values sent between devices are 32-bit elements; how exact they have to be, the bound alone decides.
No kernel may reach another device: no remote copies, remote signals or barrier semaphores. Data moves between devices by JAX's collectives and lax.ppermute only.
A program may use at most 64 MiB of HBM per device.

```python
import jax
import jax.numpy as jnp
from jax import lax

W = 256
K = 256
NS_STEPS = 4
LEAVES = 8
TOPS = 2


def draw_leaf_maps(key, part):
    matrix_size = 4 * W
    factor_key, diagonal_key = jax.random.split(key, 2)
    factors = jnp.clip(jax.random.normal(factor_key, (LEAVES, matrix_size, W), jnp.float32), -4.0, 4.0)
    gram = jnp.einsum('lik,ljk->lij', factors, factors, precision=lax.Precision.HIGHEST) * (1.5 / W)
    gram = 0.5 * (gram + jnp.swapaxes(gram, 1, 2))
    diagonal = jax.random.uniform(diagonal_key, (LEAVES, matrix_size), jnp.float32, 1.0, 2.0)
    matrix = gram + diagonal[:, :, None] * jnp.eye(matrix_size, dtype=jnp.float32)[None]
    return matrix.reshape(LEAVES * 4, W, matrix_size)


def steps_of(key, shape, shards, least, largest):
    loudness, own = 1.0, jax.random.fold_in(key, 6)
    for axis_at, shards_of in shards:
        draws = jnp.exp(jax.random.uniform(jax.random.fold_in(own, axis_at), (shards_of,), jnp.float32, least / len(shards), largest / len(shards)))
        loudness = loudness * jnp.repeat(draws, shape[axis_at] // shards_of).reshape([-1 if axis == axis_at else 1 for axis in range(len(shape))])
    return loudness


def noise(stream_key, shape, scale, limit, cuts=(), kind=jnp.bfloat16):
    loudness = steps_of(stream_key, shape, cuts, -0.22, 0.18) if cuts else 1.0
    array = jax.random.normal(stream_key, shape, jnp.float32) * scale * loudness
    return jnp.minimum(jnp.maximum(array, -limit), limit).astype(kind)


def setup_inputs(seed: int = 0) -> dict:
    key_of = jax.random.split(jax.random.key(seed), 5)
    leaf_maps = draw_leaf_maps(jax.random.fold_in(key_of[4], 71), 0)
    order_one = jax.vmap(lambda own: jax.random.permutation(own, 4))(jax.random.split(key_of[1], LEAVES)).reshape((LEAVES, 4)).astype(jnp.int32)
    order_two = jax.vmap(lambda own: jax.random.permutation(own, 6))(jax.random.split(key_of[2], (LEAVES // 2))).reshape((LEAVES // 2, 6)).astype(jnp.int32)
    top_data = noise(key_of[3], (TOPS * 8, W, K), 1.0, 6.0, ((0, 8), (1, 4)), jnp.float32)
    return dict(leaf_maps=leaf_maps, order_one=order_one, order_two=order_two, top_data=top_data)


def exact_dot(left_matrix, right_matrix):
    return jnp.dot(left_matrix, right_matrix, precision=lax.Precision.HIGHEST, preferred_element_type=jnp.float32)


def permute_map(matrix, edge_order):
    edge_count = edge_order.shape[0]
    blocks = matrix.reshape(edge_count, W, edge_count, W)
    blocks = jnp.take(blocks, edge_order, axis=0)
    blocks = jnp.take(blocks, edge_order, axis=2)
    return blocks.reshape(edge_count * W, edge_count * W)


def newton_inverse(interface_block):
    block_size = interface_block.shape[0]
    row_bound = jnp.max(jnp.sum(jnp.abs(interface_block), axis=1))
    iterate = jnp.eye(block_size, dtype=jnp.float32) / row_bound
    for iteration in range(NS_STEPS):
        iterate = 2.0 * iterate - exact_dot(exact_dot(interface_block, iterate), iterate)
    return iterate


def merge_pair(first_map, second_map, first_order, second_order, inner_edges):
    edge_count = first_order.shape[0]
    outer_size = (edge_count - inner_edges) * W
    first_perm = permute_map(first_map, first_order)
    second_perm = permute_map(second_map, second_order)
    interface_block = first_perm[outer_size:, outer_size:] + second_perm[outer_size:, outer_size:]
    inverse = newton_inverse(interface_block)
    left_side = jnp.concatenate([first_perm[:outer_size, outer_size:], second_perm[:outer_size, outer_size:]], axis=0)
    right_side = jnp.concatenate([first_perm[outer_size:, :outer_size], second_perm[outer_size:, :outer_size]], axis=1)
    zero_block = jnp.zeros((outer_size, outer_size), jnp.float32)
    upper_rows = jnp.concatenate([first_perm[:outer_size, :outer_size], zero_block], axis=1)
    lower_rows = jnp.concatenate([zero_block, second_perm[:outer_size, :outer_size]], axis=1)
    diagonal = jnp.concatenate([upper_rows, lower_rows], axis=0)
    merged = diagonal - exact_dot(exact_dot(left_side, inverse), right_side)
    return merged, inverse, right_side


def descend_pair(node_data, inverse, right_side, first_order, second_order):
    edge_count = first_order.shape[0]
    outer_size = node_data.shape[0] // 2
    inner_data = -exact_dot(inverse, exact_dot(right_side, node_data))
    results = []
    for which_half, edge_order in ((0, first_order), (1, second_order)):
        outer_rows = node_data[which_half * outer_size:(which_half + 1) * outer_size]
        stacked = jnp.concatenate([outer_rows, inner_data], axis=0).reshape(edge_count, W, -1)
        restored = jnp.zeros_like(stacked).at[edge_order].set(stacked)
        results.append(restored.reshape(edge_count * W, -1))
    return results


def reference(leaf_maps, order_one, order_two, top_data):
    leaf_count = order_one.shape[0]
    leaf_list = leaf_maps.reshape(leaf_count, 4 * W, 4 * W)
    node_maps, node_inverses, node_rights = [], [], []
    for pair_index in range(leaf_count // 2):
        merged, inverse, right_side = merge_pair(leaf_list[2 * pair_index], leaf_list[2 * pair_index + 1], order_one[2 * pair_index], order_one[2 * pair_index + 1], 1)
        node_maps.append(merged)
        node_inverses.append(inverse)
        node_rights.append(right_side)
    top_maps, top_inverses, top_rights = [], [], []
    for quad_index in range(leaf_count // 4):
        merged, inverse, right_side = merge_pair(node_maps[2 * quad_index], node_maps[2 * quad_index + 1], order_two[2 * quad_index], order_two[2 * quad_index + 1], 2)
        top_maps.append(merged)
        top_inverses.append(inverse)
        top_rights.append(right_side)
    top_map = jnp.stack(top_maps).reshape(leaf_count * 2, W, 8 * W)
    top_columns = top_data.reshape(leaf_count // 4, 8 * W, K)
    leaf_parts = []
    for quad_index in range(leaf_count // 4):
        first_data, second_data = descend_pair(top_columns[quad_index], top_inverses[quad_index], top_rights[quad_index], order_two[2 * quad_index], order_two[2 * quad_index + 1])
        for node_index, node_data in ((2 * quad_index, first_data), (2 * quad_index + 1, second_data)):
            first_leaf, second_leaf = descend_pair(node_data, node_inverses[node_index], node_rights[node_index], order_one[2 * node_index], order_one[2 * node_index + 1])
            leaf_parts.append(first_leaf)
            leaf_parts.append(second_leaf)
    leaf_data = jnp.stack(leaf_parts).reshape(leaf_count * 4, W, K)
    return top_map, leaf_data
```

```python
import jax
import jax.numpy as jnp
from jax import lax
from jax.experimental import pallas as pl
from jax.experimental.pallas import tpu as pltpu
from jax.sharding import PartitionSpec as P

W = 256
K = 256
F32 = jnp.float32
BF16 = jnp.bfloat16
NN = (((1,), (0,)), ((), ()))
NT = (((1,), (1,)), ((), ()))
TN = (((0,), (0,)), ((), ()))


def swapped(value, axis, mask):
    pairs = [(source, source ^ mask) for source in range(lax.axis_size(axis))]
    return lax.ppermute(value, axis, pairs)


def parts_of(value):
    high = value.astype(BF16)
    return high, (value - high.astype(F32)).astype(BF16)


def product(left, right, dims=NN):
    left_high, left_low = left if isinstance(left, tuple) else parts_of(left)
    right_high, right_low = right if isinstance(right, tuple) else parts_of(right)

    def one(a, b):
        return lax.dot_general(a, b, dims, preferred_element_type=F32)

    return one(left_high, right_low) + one(left_low, right_high) + one(left_high, right_high)


def newton(block):
    size = block.shape[0]
    bound = jnp.max(jnp.sum(jnp.abs(block), axis=1, keepdims=True), axis=0, keepdims=True)
    inverse_bound = 1.0 / bound
    rows = lax.broadcasted_iota(jnp.int32, (size, size), 0)
    columns = lax.broadcasted_iota(jnp.int32, (size, size), 1)
    eye = (rows == columns).astype(F32)
    power = eye - block * inverse_bound
    total = (eye + power) * inverse_bound
    split = parts_of(power)
    for _ in range(3):
        power = product(split, split)
        split = parts_of(power)
        total = total + product(total, split)
    return total


class Tree:
    def __init__(self, index, order_one, order_two):
        self.leaf = index[0]
        self.member = index[1]
        self.half = self.leaf % 2
        self.node = self.leaf // 2
        self.order_one = order_one
        self.order_two = order_two

    def edge(self, position):
        joint = self.order_two[self.node, position]
        which = joint // 3
        return which, self.order_one[2 * self.node + which, joint % 3]

    def inner(self, which):
        return self.order_one[2 * self.node + which, 3]


def block_of(tree, own, other, which, row_edge, start, size, column_edge):
    column = pl.ds(pl.multiple_of(column_edge * W, W), W)
    rows = pl.ds(start, size)
    return jnp.where(which == tree.half, own[row_edge, rows, column], other[row_edge, rows, column])


def first_kernel(index, order_one, order_two, own, other, piece, coupling):
    tree = Tree(index, order_one, order_two)
    half_width = piece.shape[1]
    width = coupling.shape[1]
    start = pl.multiple_of(tree.half * half_width, half_width)
    total = None
    for which in range(2):
        inner = tree.inner(which)
        part = block_of(tree, own, other, which, inner, start, half_width, inner)
        total = part if total is None else total + part
    piece[0] = total
    for slot in range(2):
        which, edge = tree.edge(4 + slot)
        piece[1 + slot] = block_of(tree, own, other, which, edge, start, half_width, tree.inner(which))
    for slot in range(2):
        which, edge = tree.edge(2 * tree.half + slot)
        coupling[slot] = block_of(tree, own, other, which, edge, 0, width, tree.inner(which))


def interface_rows(tree, own, other, position, start, size):
    which, edge = tree.edge(position)
    found = []
    for slot in range(2):
        column_which, column_edge = tree.edge(4 + slot)
        value = block_of(tree, own, other, which, edge, start, size, column_edge)
        found.append(jnp.where(which == column_which, value, 0.0))
    return jnp.concatenate(found, axis=1)


def second_kernel(count, index, order_one, order_two, own, other, coupling, *refs):
    pieces, (inner_rows, outer_rows, inverse_out, coupling_inner, sums) = refs[: 2 * count], refs[2 * count :]
    tree = Tree(index, order_one, order_two)
    half_width = pieces[0].shape[1]
    width = 2 * half_width
    for mask in range(count):
        for side in range(2):
            piece = pieces[2 * mask + side]
            row = (tree.member ^ mask) * width + (tree.half ^ side) * half_width
            sums[pl.ds(pl.multiple_of(row, half_width), half_width), :] = piece[0]
            for slot in range(2):
                target = pl.ds(pl.multiple_of(row + slot * W, half_width), half_width)
                coupling_inner[target, :] = piece[1 + slot]
    inverse = newton(sums[...])
    inverse_out[...] = inverse
    right = parts_of(product(inverse, coupling_inner[...], NT))
    start = pl.multiple_of(tree.half * half_width, half_width)
    for slot in range(2):
        base = interface_rows(tree, own, other, 4 + slot, start, half_width)
        inner_rows[slot * half_width : (slot + 1) * half_width, :] = base - product(pieces[0][1 + slot], right)
    for slot in range(2):
        base = interface_rows(tree, own, other, 2 * tree.half + slot, 0, width)
        outer_rows[slot * width : (slot + 1) * width, :] = base - product(coupling[slot], right)


def third_kernel(count, index, *refs):
    pieces, (inverse_out, sums) = refs[: 2 * count], refs[2 * count :]
    half, member = index[0] % 2, index[1]
    half_width = pieces[0].shape[0] // 2
    width = 2 * half_width
    for mask in range(count):
        for side in range(2):
            piece = pieces[2 * mask + side]
            row = (member ^ mask) * width + (half ^ side) * half_width
            for slot in range(2):
                target = pl.ds(pl.multiple_of(row + slot * W, half_width), half_width)
                sums[target, :] = piece[slot * half_width : (slot + 1) * half_width, :]
    inverse_out[...] = newton(sums[...])


def fourth_kernel(count, index, order_one, order_two, own, other, coupling_inner, inverse_one, inverse_two, *refs):
    couplings, refs = refs[: 2 * count], refs[2 * count :]
    outers, refs = refs[: 4 * count], refs[4 * count :]
    datas, refs = refs[: 4 * count], refs[4 * count :]
    top_map, leaf_data, coupling, outer, data, inner = refs
    tree = Tree(index, order_one, order_two)
    node_bit = tree.node % 2
    width = own.shape[1]
    for mask in range(count):
        at = (tree.member ^ mask) * width
        for side in range(2):
            first = 2 * (tree.half ^ side)
            for slot in range(2):
                row = pl.multiple_of((first + slot) * W + at, width)
                coupling[pl.ds(row, width), :] = couplings[2 * mask + side][slot]
                for far in range(2):
                    row = pl.multiple_of((4 * (node_bit ^ far) + first + slot) * W + at, width)
                    source = 4 * mask + 2 * far + side
                    outer[pl.ds(row, width), :] = outers[source][slot * width : (slot + 1) * width, :]
                    data[pl.ds(row, width), :] = datas[source][slot]
    second = parts_of(inverse_two[...])
    outer_all = parts_of(outer[...])
    scaled = product(outers[0][...], second)
    change = product(scaled, outer_all, NT)
    coupling_all = parts_of(coupling[...])
    first_inverse = parts_of(inverse_one[...])
    near = pl.multiple_of(node_bit * 4 * W, W)
    for slot in range(2):
        position = 2 * tree.half + slot
        which, edge = tree.edge(position)
        rows = slice(slot * width, (slot + 1) * width)
        top_map[slot] = -change[rows]
        local = product(product(couplings[0][slot], first_inverse), coupling_all, NT)
        for column in range(4):
            column_which, column_edge = tree.edge(column)
            value = block_of(tree, own, other, which, edge, 0, width, column_edge)
            value = jnp.where(which == column_which, value, 0.0) - local[:, column * W : (column + 1) * W]
            target = pl.ds(pl.multiple_of(near + column * W, W), W)
            top_map[slot, :, target] = top_map[slot, :, target] + value
    driven = product(outer_all, data[...], TN)
    inner[...] = -product(second, driven)
    near_data = data[pl.ds(near, 4 * W), :]
    driven = product(coupling_all, near_data, TN) + product(coupling_inner[...], inner[...], TN)
    mine = pl.multiple_of(tree.member * width, width)
    leaf_data[tree.order_one[tree.leaf, 3]] = -product(inverse_one[pl.ds(mine, width), :], driven)
    for slot in range(3):
        joint = 3 * tree.half + slot
        position = 0
        for place in range(6):
            position = position + place * (order_two[tree.node, place] == joint).astype(jnp.int32)
        from_data = data[pl.ds(pl.multiple_of(near + jnp.minimum(position, 3) * W + mine, width), width), :]
        from_inner = inner[pl.ds(pl.multiple_of(jnp.maximum(position - 4, 0) * W + mine, width), width), :]
        leaf_data[order_one[tree.leaf, slot]] = jnp.where(position < 4, from_data, from_inner)


def call(kernel, name, scalar_count, outs, scratch, *args):
    smem = pl.BlockSpec(memory_space=pltpu.SMEM)
    vmem = pl.BlockSpec(memory_space=pltpu.VMEM)
    return pl.pallas_call(
        kernel,
        name=name,
        in_specs=[smem] * scalar_count + [vmem] * (len(args) - scalar_count),
        out_specs=[vmem] * len(outs),
        out_shape=[jax.ShapeDtypeStruct(shape, F32) for shape in outs],
        scratch_shapes=[pltpu.VMEM(shape, F32) for shape in scratch],
        compiler_params=pltpu.CompilerParams(vmem_limit_bytes=56 * 2**20),
    )(*args)


def shards(leaf_maps, order_one, order_two, top_data):
    width = leaf_maps.shape[1]
    half_width = width // 2
    count = lax.axis_size("sub")
    bits = [("sub", 2**bit) for bit in range((count - 1).bit_length())] + [("leaf", 2)]
    index = jnp.stack([lax.axis_index("leaf"), lax.axis_index("sub")]).astype(jnp.int32)

    def across(value):
        return [value if mask == 0 else swapped(value, "sub", mask) for mask in range(count)]

    def spread(value, used):
        found = {0: value}
        for mask in sorted(range(1, 2 ** len(used)), key=lambda m: (bin(m).count("1"), m)):
            held = [bit for bit in range(len(used)) if mask >> bit & 1]
            chosen = next((bit for bit in held if (bit + 1) % len(used) in held), held[0])
            found[mask] = swapped(found[mask ^ (1 << chosen)], *used[chosen])
        return [found[mask] for mask in range(2 ** len(used))]

    def with_sibling(values):
        return [item for value in values for item in (value, swapped(value, "leaf", 1))]

    other = swapped(leaf_maps, "leaf", 1)
    piece, coupling = call(
        first_kernel, "first", 3, [(3, half_width, W), (2, width, W)], [],
        index, order_one, order_two, leaf_maps, other,
    )
    pieces = with_sibling(across(piece))
    datas = spread(top_data, bits)
    couplings = with_sibling(spread(coupling, bits[:-1]))
    inner_rows, outer_rows, inverse_one, coupling_inner = call(
        lambda *refs: second_kernel(count, *refs), "second", 3,
        [(2 * half_width, 2 * W), (2 * width, 2 * W), (W, W), (2 * W, W)], [(W, W)],
        index, order_one, order_two, leaf_maps, other, coupling, *pieces,
    )
    summed = inner_rows + swapped(inner_rows, "leaf", 2)
    (inverse_two,) = call(
        lambda *refs: third_kernel(count, *refs), "third", 1, [(2 * W, 2 * W)], [(2 * W, 2 * W)],
        index, *with_sibling(across(summed)),
    )
    outers = spread(outer_rows, bits)

    def far_last(values):
        ordered = [values[mask + far * count] for mask in range(count) for far in range(2)]
        return with_sibling(ordered)

    top_map, leaf_data = call(
        lambda *refs: fourth_kernel(count, *refs), "fourth", 3,
        [(2, width, 8 * W), (4, width, K)],
        [(4 * W, W), (8 * W, 2 * W), (8 * W, K), (2 * W, K)],
        index, order_one, order_two, leaf_maps, other, coupling_inner, inverse_one, inverse_two,
        *couplings, *far_last(outers), *far_last(datas),
    )
    return (top_map, leaf_data)


def solution(mesh):
    in_specs = (P("leaf", "sub", None), P(), P(), P("leaf", "sub", None))
    out_specs = (P("leaf", "sub", None), P("leaf", "sub", None))
    return jax.shard_map(shards, mesh=mesh, in_specs=in_specs, out_specs=out_specs, check_vma=False)
```

```python
import jax
import jax.numpy as jnp
from jax import lax
from jax.experimental import pallas as pl
from jax.experimental.pallas import tpu as pltpu
from jax.sharding import PartitionSpec as P


W = 256
K = 256
F32 = jnp.float32
BF16 = jnp.bfloat16
NN = (((1,), (0,)), ((), ()))
NT = (((1,), (1,)), ((), ()))

VMEM_MIB = 24


def swapped(value, axis, mask):
    pairs = [(source, source ^ mask) for source in range(lax.axis_size(axis))]
    return lax.ppermute(value, axis, pairs)


def parts_of(value):
    high = value.astype(BF16)
    return high, (value - high.astype(F32)).astype(BF16)


def product(left, right, dims=NN):
    left_high, left_low = left if isinstance(left, tuple) else parts_of(left)
    right_high, right_low = right if isinstance(right, tuple) else parts_of(right)

    def one(a, b):
        return lax.dot_general(a, b, dims, preferred_element_type=F32)

    return one(left_high, right_low) + one(left_low, right_high) + one(left_high, right_high)


def newton(block):
    size = block.shape[0]
    bound = jnp.max(jnp.sum(jnp.abs(block), axis=1, keepdims=True), axis=0, keepdims=True)
    inverse_bound = 1.0 / bound
    rows = lax.broadcasted_iota(jnp.int32, (size, size), 0)
    columns = lax.broadcasted_iota(jnp.int32, (size, size), 1)
    eye = (rows == columns).astype(F32)
    power = eye - block * inverse_bound
    total = (eye + power) * inverse_bound
    split = parts_of(power)
    for _ in range(3):
        power = product(split, split)
        split = parts_of(power)
        total = total + product(total, split)
    return total


class Tree:
    def __init__(self, order_one, order_two):
        self.leaf = lax.axis_index("leaf")
        self.member = lax.axis_index("sub")
        self.half = self.leaf % 2
        self.node = self.leaf // 2
        self.order_one = order_one
        self.order_two = order_two

    def edge(self, position):
        joint = self.order_two[self.node, position]
        which = joint // 3
        return which, self.order_one[2 * self.node + which, joint % 3]

    def inner(self, which):
        return self.order_one[2 * self.node + which, 3]


def block_of(tree, own, other, which, row_edge, start, size, column_edge):
    column = pl.ds(pl.multiple_of(column_edge * W, W), W)
    rows = pl.ds(start, size)
    return jnp.where(which == tree.half, own[row_edge, rows, column], other[row_edge, rows, column])


def first_kernel(order_one, order_two, own, other, piece, coupling, coupling_own):
    tree = Tree(order_one, order_two)
    half_width = piece.shape[1]
    width = coupling.shape[1]
    start = pl.multiple_of(tree.half * half_width, half_width)
    total = None
    for which in range(2):
        inner = tree.inner(which)
        part = block_of(tree, own, other, which, inner, start, half_width, inner)
        total = part if total is None else total + part
    piece[0] = total
    for slot in range(2):
        which, edge = tree.edge(4 + slot)
        piece[1 + slot] = block_of(tree, own, other, which, edge, start, half_width, tree.inner(which))
    for slot in range(4):
        which, edge = tree.edge(slot)
        coupling[slot] = block_of(tree, own, other, which, edge, 0, width, tree.inner(which))
    for slot in range(2):
        coupling_own[slot] = coupling[2 * tree.half + slot]


def interface_rows(tree, own, other, position, start, size):
    which, edge = tree.edge(position)
    found = []
    for slot in range(2):
        column_which, column_edge = tree.edge(4 + slot)
        value = block_of(tree, own, other, which, edge, start, size, column_edge)
        found.append(jnp.where(which == column_which, value, 0.0))
    return jnp.concatenate(found, axis=1)


def second_kernel(count, order_one, order_two, own, other, *refs):
    pieces, (inner_rows, inverse_out, coupling_inner, right_out, sums) = refs[: 2 * count], refs[2 * count :]
    tree = Tree(order_one, order_two)
    half_width = pieces[0].shape[1]
    width = 2 * half_width
    for mask in range(count):
        for side in range(2):
            piece = pieces[2 * mask + side]
            row = (tree.member ^ mask) * width + (tree.half ^ side) * half_width
            sums[pl.ds(pl.multiple_of(row, half_width), half_width), :] = piece[0]
            for slot in range(2):
                target = pl.ds(pl.multiple_of(row + slot * W, half_width), half_width)
                coupling_inner[target, :] = piece[1 + slot]
    inverse = newton(sums[...])
    inverse_out[...] = inverse
    right = product(inverse, coupling_inner[...], NT)
    right_out[...] = right
    start = pl.multiple_of(tree.half * half_width, half_width)
    left = jnp.concatenate([pieces[0][1], pieces[0][2]], axis=0)
    change = product(left, right)
    for slot in range(2):
        rows = slice(slot * half_width, (slot + 1) * half_width)
        inner_rows[rows, :] = interface_rows(tree, own, other, 4 + slot, start, half_width) - change[rows]


def outer_kernel(order_one, order_two, own, other, coupling, right, outer_all, outer_own):
    tree = Tree(order_one, order_two)
    width = coupling.shape[1]
    change = product(coupling[...].reshape(4 * width, W), right[...])
    for slot in range(4):
        base = interface_rows(tree, own, other, slot, 0, width)
        outer_all[slot] = base - change[slot * width : (slot + 1) * width]
    for slot in range(2):
        outer_own[slot] = outer_all[2 * tree.half + slot]


def third_kernel(count, *refs):
    pieces, (inverse_out, sums) = refs[: 2 * count], refs[2 * count :]
    half, member = lax.axis_index("leaf") % 2, lax.axis_index("sub")
    half_width = pieces[0].shape[0] // 2
    width = 2 * half_width
    for mask in range(count):
        for side in range(2):
            piece = pieces[2 * mask + side]
            row = (member ^ mask) * width + (half ^ side) * half_width
            for slot in range(2):
                target = pl.ds(pl.multiple_of(row + slot * W, half_width), half_width)
                sums[target, :] = piece[slot * half_width : (slot + 1) * half_width, :]
    inverse_out[...] = newton(sums[...])


def near_kernel(count, order_one, order_two, own, other, coupling, inverse_one, *refs):
    bulks, (base_out, driven_one, coupling_half, data_half) = refs[:count], refs[count:]
    tree = Tree(order_one, order_two)
    node_bit = tree.node % 2
    width = own.shape[1]
    for mask in range(count):
        at = (tree.member ^ mask) * width
        for slot in range(2):
            row = pl.multiple_of(slot * W + at, width)
            coupling_half[pl.ds(row, width), :] = bulks[mask][4 + slot]
            for far in range(2):
                row = pl.multiple_of((2 * (node_bit ^ far) + slot) * W + at, width)
                data_half[pl.ds(row, width), :] = bulks[mask][2 * far + slot]
    coupling_split = parts_of(coupling_half[...])
    scaled = product(coupling[...].reshape(4 * width, W), inverse_one[...])
    local = product(scaled, coupling_split, NT)
    for slot in range(4):
        which, edge = tree.edge(slot)
        for column in range(2):
            column_which, column_edge = tree.edge(2 * tree.half + column)
            value = block_of(tree, own, other, which, edge, 0, width, column_edge)
            value = jnp.where(which == column_which, value, 0.0)
            rows, columns = slice(slot * width, (slot + 1) * width), slice(column * W, (column + 1) * W)
            base_out[slot, :, columns] = value - local[rows, columns]
    near = data_half[pl.ds(pl.multiple_of(node_bit * 2 * W, W), 2 * W), :]
    driven_one[...] = product(near.T, coupling_split)


def far_kernel(count, data_half, driven_one, *refs):
    outers, (driven, outer_half) = refs[: 2 * count], refs[2 * count :]
    node_bit, member = (lax.axis_index("leaf") // 2) % 2, lax.axis_index("sub")
    width = outers[0].shape[1]
    for mask in range(count):
        at = (member ^ mask) * width
        for slot in range(2):
            for far in range(2):
                row = pl.multiple_of((2 * (node_bit ^ far) + slot) * W + at, width)
                outer_half[pl.ds(row, width), :] = outers[mask + far * count][slot]
    driven[:, : 2 * W] = product(data_half[...].T, outer_half[...])
    driven[:, 2 * W :] = driven_one[...]


def top_kernel(base, outer_all, inverse_two, outer_half, mine, theirs):
    half, node_bit = lax.axis_index("leaf") % 2, (lax.axis_index("leaf") // 2) % 2
    slots, width, columns = base.shape
    scaled = product(outer_all[...].reshape(slots * width, columns), inverse_two[...])
    change = -product(scaled, outer_half[...], NT)
    for bit in range(2):
        held = jnp.where(bit == node_bit, base[...], 0.0)
        part = held + change[:, bit * columns : (bit + 1) * columns].reshape(slots, width, columns)
        mine[:, :, bit * columns : (bit + 1) * columns] = jnp.where(half == 0, part[:2], part[2:])
        theirs[:, :, bit * columns : (bit + 1) * columns] = jnp.where(half == 0, part[2:], part[:2])


def leaf_kernel(order_one, order_two, data_own, data_other, coupling_inner, inverse_one, inverse_two, driven, driven_other, leaf_data, inner):
    tree = Tree(order_one, order_two)
    width = leaf_data.shape[1]
    total = driven[...] + driven_other[...]
    second = parts_of(total[:, : 2 * W])
    lifted = -product(second, inverse_two[...])
    first = total[:, 2 * W :] + product(lifted, coupling_inner[...])
    mine = pl.multiple_of(tree.member * width, width)
    rows = [inverse_two[pl.ds(pl.multiple_of(slot * W + mine, width), width), :] for slot in range(2)]
    inner[...] = -product(jnp.concatenate(rows, axis=0), second, NT)
    leaf_data[tree.order_one[tree.leaf, 3]] = -product(inverse_one[pl.ds(mine, width), :], first, NT)
    for slot in range(3):
        joint = 3 * tree.half + slot
        position = 0
        for place in range(6):
            position = position + place * (order_two[tree.node, place] == joint).astype(jnp.int32)
        place = position % 2
        from_data = jnp.where(position // 2 == tree.half, data_own[place], data_other[place])
        from_inner = inner[pl.ds(pl.multiple_of(place * width, width), width), :]
        leaf_data[order_one[tree.leaf, slot]] = jnp.where(position < 4, from_data, from_inner)


def join_kernel(mine, theirs, top_map):
    half = lax.axis_index("leaf") % 2
    columns = mine.shape[2] // 2
    for bit in range(2):
        source = slice(bit * columns, (bit + 1) * columns)
        for side, held in enumerate((mine, theirs)):
            target = pl.multiple_of((2 * bit + (half ^ side)) * columns, columns)
            top_map[:, :, pl.ds(target, columns)] = held[:, :, source]


def call(kernel, scalar_count, outs, scratch, *args):
    smem = pl.BlockSpec(memory_space=pltpu.SMEM)
    vmem = pl.BlockSpec(memory_space=pltpu.VMEM)
    return pl.pallas_call(
        kernel,
        in_specs=[smem] * scalar_count + [vmem] * (len(args) - scalar_count),
        out_specs=[vmem] * len(outs),
        out_shape=[jax.ShapeDtypeStruct(shape, F32) for shape in outs],
        scratch_shapes=[pltpu.VMEM(shape, F32) for shape in scratch],
        compiler_params=pltpu.CompilerParams(vmem_limit_bytes=VMEM_MIB * 2**20),
    )(*args)


def shards(leaf_maps, order_one, order_two, top_data):
    width = leaf_maps.shape[1]
    half_width = width // 2
    count = lax.axis_size("sub")
    bits = [("sub", 2**bit) for bit in range((count - 1).bit_length())] + [("leaf", 2)]
    orders = (order_one, order_two)

    def across(value):
        found = {0: value}
        for mask in sorted(range(1, count), key=lambda m: (-bin(m).count("1"), m)):
            found[mask] = swapped(value, "sub", mask)
        return [found[mask] for mask in range(count)]

    def spread(value, used):
        found = {0: value}
        for mask in sorted(range(1, 2 ** len(used)), key=lambda m: (bin(m).count("1"), m)):
            held = [bit for bit in range(len(used)) if mask >> bit & 1]
            chosen = next((bit for bit in held if (bit + 1) % len(used) in held), held[0])
            found[mask] = swapped(found[mask ^ (1 << chosen)], *used[chosen])
        return [found[mask] for mask in range(2 ** len(used))]

    def with_sibling(values):
        return [item for value in values for item in (value, swapped(value, "leaf", 1))]

    other = swapped(leaf_maps, "leaf", 1)
    data_far = swapped(top_data, "leaf", 2)
    piece, coupling, coupling_own = call(
        first_kernel, 2, [(3, half_width, W), (4, width, W), (2, width, W)], [], *orders, leaf_maps, other
    )
    pieces = with_sibling(across(piece))
    data_other = swapped(top_data, "leaf", 1)
    bulks = spread(jnp.concatenate([top_data, data_far, coupling_own], axis=0), bits[:-1])
    inner_rows, inverse_one, coupling_inner, right = call(
        lambda *refs: second_kernel(count, *refs), 2,
        [(2 * half_width, 2 * W), (W, W), (2 * W, W), (W, 2 * W)], [(W, W)],
        *orders, leaf_maps, other, *pieces,
    )
    summed = inner_rows + swapped(inner_rows, "leaf", 2)
    outer_all, outer_own = call(
        outer_kernel, 2, [(4, width, 2 * W), (2, width, 2 * W)], [], *orders, leaf_maps, other, coupling, right
    )
    outers = spread(outer_own, bits)
    (inverse_two,) = call(
        lambda *refs: third_kernel(count, *refs), 0, [(2 * W, 2 * W)], [(2 * W, 2 * W)],
        *with_sibling(across(summed)),
    )
    base, driven_one, _, data_half = call(
        lambda *refs: near_kernel(count, *refs), 2,
        [(4, width, 2 * W), (K, W), (2 * W, W), (4 * W, K)], [], *orders, leaf_maps, other, coupling, inverse_one, *bulks,
    )
    driven, outer_half = call(
        lambda *refs: far_kernel(count, *refs), 0, [(K, 3 * W), (4 * W, 2 * W)], [], data_half, driven_one, *outers
    )
    driven_other = swapped(driven, "leaf", 1)
    mine, theirs = call(top_kernel, 0, [(2, width, 4 * W)] * 2, [], base, outer_all, inverse_two, outer_half)
    received = swapped(theirs, "leaf", 1)
    (leaf_data,) = call(
        leaf_kernel, 2, [(4, width, K)], [(2 * width, K)],
        *orders, top_data, data_other, coupling_inner, inverse_one, inverse_two, driven, driven_other,
    )
    (top_map,) = call(join_kernel, 0, [(2, width, 8 * W)], [], mine, received)
    return (top_map, leaf_data)


def solution(mesh):
    in_specs = (P("leaf", "sub", None), P(), P(), P("leaf", "sub", None))
    out_specs = (P("leaf", "sub", None), P("leaf", "sub", None))

    return jax.shard_map(shards, mesh=mesh, in_specs=in_specs, out_specs=out_specs, check_vma=False)
```

```python
import jax
import jax.numpy as jnp
from jax import lax
from jax.experimental import pallas as pl
from jax.experimental.pallas import tpu as pltpu
from jax.sharding import PartitionSpec as P


W = 256
K = 256
F32 = jnp.float32
BF16 = jnp.bfloat16
NN = (((1,), (0,)), ((), ()))
NT = (((1,), (1,)), ((), ()))

VMEM_MIB = 24


def swapped(value, axis, mask):
    pairs = [(source, source ^ mask) for source in range(lax.axis_size(axis))]
    return lax.ppermute(value, axis, pairs)


def parts_of(value):
    high = value.astype(BF16)
    return high, (value - high.astype(F32)).astype(BF16)


def product(left, right, dims=NN):
    left_high, left_low = left if isinstance(left, tuple) else parts_of(left)
    right_high, right_low = right if isinstance(right, tuple) else parts_of(right)

    def one(a, b):
        return lax.dot_general(a, b, dims, preferred_element_type=F32)

    return one(left_high, right_low) + one(left_low, right_high) + one(left_high, right_high)


def newton(block):
    size = block.shape[0]
    bound = jnp.max(jnp.sum(jnp.abs(block), axis=1, keepdims=True), axis=0, keepdims=True)
    inverse_bound = 1.0 / bound
    rows = lax.broadcasted_iota(jnp.int32, (size, size), 0)
    columns = lax.broadcasted_iota(jnp.int32, (size, size), 1)
    eye = (rows == columns).astype(F32)
    power = eye - block * inverse_bound
    total = (eye + power) * inverse_bound
    split = parts_of(power)
    for _ in range(3):
        power = product(split, split)
        split = parts_of(power)
        total = total + product(total, split)
    return total


class Tree:
    def __init__(self, order_one, order_two):
        self.leaf = lax.axis_index("leaf")
        self.member = lax.axis_index("sub")
        self.half = self.leaf % 2
        self.node = self.leaf // 2
        self.order_one = order_one
        self.order_two = order_two

    def edge(self, position):
        joint = self.order_two[self.node, position]
        which = joint // 3
        return which, self.order_one[2 * self.node + which, joint % 3]

    def inner(self, which):
        return self.order_one[2 * self.node + which, 3]


def block_of(tree, own, other, which, row_edge, start, size, column_edge):
    column = pl.ds(pl.multiple_of(column_edge * W, W), W)
    rows = pl.ds(start, size)
    return jnp.where(which == tree.half, own[row_edge, rows, column], other[row_edge, rows, column])


def first_kernel(order_one, order_two, own, other, data, piece, coupling, bulk):
    tree = Tree(order_one, order_two)
    half_width = piece.shape[1]
    width = coupling.shape[1]
    start = pl.multiple_of(tree.half * half_width, half_width)
    total = None
    for which in range(2):
        inner = tree.inner(which)
        part = block_of(tree, own, other, which, inner, start, half_width, inner)
        total = part if total is None else total + part
    piece[0] = total
    for slot in range(2):
        which, edge = tree.edge(4 + slot)
        piece[1 + slot] = block_of(tree, own, other, which, edge, start, half_width, tree.inner(which))
    for slot in range(4):
        which, edge = tree.edge(slot)
        coupling[slot] = block_of(tree, own, other, which, edge, 0, width, tree.inner(which))
    same, inner_leaf, outer_leaf = packing(tree, tree.node)
    holder = jnp.where(outer_leaf[0] == inner_leaf[0], 0, 1)
    for slot in range(2):
        bulk[slot] = data[slot]
        bulk[2 + slot] = coupling[2 * tree.half + slot]
        row = jnp.where(same, holder, slot)
        column = jnp.where(same, slot, jnp.where(outer_leaf[slot] == inner_leaf[0], 0, 1))
        which, edge = tree.edge(2 * tree.half + row)
        _, column_edge = tree.edge(4 + column)
        bulk[4 + slot] = block_of(tree, own, other, which, edge, 0, width, column_edge)


def packing(tree, node):
    inner_leaf = [tree.order_two[node, 4 + slot] // 3 for slot in range(2)]
    outer_leaf = [tree.order_two[node, 2 * tree.half + slot] // 3 for slot in range(2)]
    return inner_leaf[0] == inner_leaf[1], inner_leaf, outer_leaf


def interface_rows(tree, own, other, position, start, size):
    which, edge = tree.edge(position)
    found = []
    for slot in range(2):
        column_which, column_edge = tree.edge(4 + slot)
        value = block_of(tree, own, other, which, edge, start, size, column_edge)
        found.append(jnp.where(which == column_which, value, 0.0))
    return jnp.concatenate(found, axis=1)


def second_kernel(count, order_one, order_two, own, other, *refs):
    pieces, outs = refs[: 2 * count], refs[2 * count :]
    inner_rows, inverse_out, coupling_inner, right_out, right_half, sums = outs
    tree = Tree(order_one, order_two)
    half_width = pieces[0].shape[1]
    width = 2 * half_width
    for mask in range(count):
        for side in range(2):
            piece = pieces[2 * mask + side]
            row = (tree.member ^ mask) * width + (tree.half ^ side) * half_width
            sums[pl.ds(pl.multiple_of(row, half_width), half_width), :] = piece[0]
            for slot in range(2):
                target = pl.ds(pl.multiple_of(row + slot * W, half_width), half_width)
                coupling_inner[target, :] = piece[1 + slot]
    inverse = newton(sums[...])
    inverse_out[...] = inverse
    right = product(inverse, coupling_inner[...], NT)
    right_out[...] = right
    right_half[...] = right_out[pl.ds(pl.multiple_of(tree.half * (W // 2), W // 2), W // 2), :]
    start = pl.multiple_of(tree.half * half_width, half_width)
    left = jnp.concatenate([pieces[0][1], pieces[0][2]], axis=0)
    change = product(left, right)
    for slot in range(2):
        rows = slice(slot * half_width, (slot + 1) * half_width)
        inner_rows[rows, :] = interface_rows(tree, own, other, 4 + slot, start, half_width) - change[rows]


def outer_kernel(order_one, order_two, own, other, coupling, right, outer_all):
    tree = Tree(order_one, order_two)
    width = coupling.shape[1]
    change = product(coupling[...].reshape(4 * width, W), right[...])
    for slot in range(4):
        base = interface_rows(tree, own, other, slot, 0, width)
        outer_all[slot] = base - change[slot * width : (slot + 1) * width]


def third_kernel(count, *refs):
    pieces, (inverse_out, sums) = refs[: 2 * count], refs[2 * count :]
    half, member = lax.axis_index("leaf") % 2, lax.axis_index("sub")
    half_width = pieces[0].shape[0] // 2
    width = 2 * half_width
    for mask in range(count):
        for side in range(2):
            piece = pieces[2 * mask + side]
            row = (member ^ mask) * width + (half ^ side) * half_width
            for slot in range(2):
                target = pl.ds(pl.multiple_of(row + slot * W, half_width), half_width)
                sums[target, :] = piece[slot * half_width : (slot + 1) * half_width, :]
    inverse_out[...] = newton(sums[...])


def gathered(tree, bulks, data_half, coupling_half, packed_zero, packed_one):
    width = bulks[0].shape[1]
    for mask, bulk in enumerate(bulks):
        at = (tree.member ^ mask) * width
        for slot in range(2):
            target = pl.ds(pl.multiple_of(slot * W + at, width), width)
            data_half[target, :] = bulk[slot]
            coupling_half[target, :] = bulk[2 + slot]
        target = pl.ds(pl.multiple_of(at, width), width)
        packed_zero[target, :] = bulk[4]
        packed_one[target, :] = bulk[5]


def outer_rows(tree, node, coupling_split, packed_zero, packed_one, right, outer_half):
    same, inner_leaf, outer_leaf = packing(tree, node)
    packed = (packed_zero, packed_one)
    change = product(coupling_split, right)
    for slot in range(2):
        rows = slice(slot * W, (slot + 1) * W)
        for column in range(2):
            columns = slice(column * W, (column + 1) * W)
            value = jnp.where(same, packed[column][...], packed[slot][...])
            value = jnp.where(outer_leaf[slot] == inner_leaf[column], value, 0.0)
            outer_half[rows, columns] = value - change[rows, columns]


def near_kernel(count, order_one, order_two, own, other, coupling, inverse_one, right, *refs):
    bulks, outs = refs[:count], refs[count:]
    base_out, outer_half, driven, coupling_half, data_half, packed_zero, packed_one = outs
    tree = Tree(order_one, order_two)
    width = own.shape[1]
    gathered(tree, bulks, data_half, coupling_half, packed_zero, packed_one)
    coupling_split = parts_of(coupling_half[...])
    scaled = product(coupling[...].reshape(4 * width, W), inverse_one[...])
    local = product(scaled, coupling_split, NT)
    for slot in range(4):
        which, edge = tree.edge(slot)
        for column in range(2):
            column_which, column_edge = tree.edge(2 * tree.half + column)
            value = block_of(tree, own, other, which, edge, 0, width, column_edge)
            value = jnp.where(which == column_which, value, 0.0)
            rows, columns = slice(slot * width, (slot + 1) * width), slice(column * W, (column + 1) * W)
            base_out[slot, :, columns] = value - local[rows, columns]
    outer_rows(tree, tree.node, coupling_split, packed_zero, packed_one, right[...], outer_half)
    turned = parts_of(data_half[...].T)
    driven[:, : 2 * W] = product(turned, outer_half[...])
    driven[:, 2 * W :] = product(turned, coupling_split)


def far_kernel(count, order_one, order_two, driven_near, right_mine, right_other, *refs):
    bulks, outs = refs[:count], refs[count:]
    outer_half, driven, coupling_half, data_half, packed_zero, packed_one, right = outs
    tree = Tree(order_one, order_two)
    gathered(tree, bulks, data_half, coupling_half, packed_zero, packed_one)
    for side, held in enumerate((right_mine, right_other)):
        right[pl.ds(pl.multiple_of((tree.half ^ side) * (W // 2), W // 2), W // 2), :] = held[...]
    node = tree.node ^ 1
    outer_rows(tree, node, parts_of(coupling_half[...]), packed_zero, packed_one, right[...], outer_half)
    driven[:, : 2 * W] = driven_near[:, : 2 * W] + product(data_half[...].T, outer_half[...])
    driven[:, 2 * W :] = driven_near[:, 2 * W :]


def top_kernel(base, outer_all, inverse_two, outer_near, outer_far, mine, theirs):
    half = lax.axis_index("leaf") % 2
    slots, width, columns = base.shape
    scaled = parts_of(product(outer_all[...].reshape(slots * width, columns), inverse_two[...]))
    for far, outer in enumerate((outer_near, outer_far)):
        part = -product(scaled, outer[...], NT).reshape(slots, width, columns)
        if not far:
            part = base[...] + part
        target = slice(far * columns, (far + 1) * columns)
        mine[:, :, target] = jnp.where(half == 0, part[:2], part[2:])
        theirs[:, :, target] = jnp.where(half == 0, part[2:], part[:2])


def leaf_kernel(order_one, order_two, data_own, data_other, coupling_inner, inverse_one, inverse_two, driven, driven_other, leaf_data, inner):
    tree = Tree(order_one, order_two)
    width = leaf_data.shape[1]
    total = driven[...] + driven_other[...]
    second = parts_of(total[:, : 2 * W])
    lifted = -product(second, inverse_two[...])
    first = total[:, 2 * W :] + product(lifted, coupling_inner[...])
    mine = pl.multiple_of(tree.member * width, width)
    rows = [inverse_two[pl.ds(pl.multiple_of(slot * W + mine, width), width), :] for slot in range(2)]
    inner[...] = -product(jnp.concatenate(rows, axis=0), second, NT)
    leaf_data[tree.order_one[tree.leaf, 3]] = -product(inverse_one[pl.ds(mine, width), :], first, NT)
    for slot in range(3):
        joint = 3 * tree.half + slot
        position = 0
        for place in range(6):
            position = position + place * (order_two[tree.node, place] == joint).astype(jnp.int32)
        place = position % 2
        from_data = jnp.where(position // 2 == tree.half, data_own[place], data_other[place])
        from_inner = inner[pl.ds(pl.multiple_of(place * width, width), width), :]
        leaf_data[order_one[tree.leaf, slot]] = jnp.where(position < 4, from_data, from_inner)


def join_kernel(mine, theirs, top_map):
    half, node_bit = lax.axis_index("leaf") % 2, (lax.axis_index("leaf") // 2) % 2
    columns = mine.shape[2] // 2
    for far in range(2):
        source = slice(far * columns, (far + 1) * columns)
        for side, held in enumerate((mine, theirs)):
            target = pl.multiple_of((2 * (node_bit ^ far) + (half ^ side)) * columns, columns)
            top_map[:, :, pl.ds(target, columns)] = held[:, :, source]


def call(kernel, scalar_count, outs, scratch, *args):
    smem = pl.BlockSpec(memory_space=pltpu.SMEM)
    vmem = pl.BlockSpec(memory_space=pltpu.VMEM)
    return pl.pallas_call(
        kernel,
        in_specs=[smem] * scalar_count + [vmem] * (len(args) - scalar_count),
        out_specs=[vmem] * len(outs),
        out_shape=[jax.ShapeDtypeStruct(shape, F32) for shape in outs],
        scratch_shapes=[pltpu.VMEM(shape, F32) for shape in scratch],
        compiler_params=pltpu.CompilerParams(vmem_limit_bytes=VMEM_MIB * 2**20),
    )(*args)


def shards(leaf_maps, order_one, order_two, top_data):
    width = leaf_maps.shape[1]
    half_width = width // 2
    count = lax.axis_size("sub")
    bits = [("sub", 2**bit) for bit in range((count - 1).bit_length())] + [("leaf", 2)]
    orders = (order_one, order_two)

    def across(value):
        found = {0: value}
        for mask in sorted(range(1, count), key=lambda m: (-bin(m).count("1"), m)):
            found[mask] = swapped(value, "sub", mask)
        return [found[mask] for mask in range(count)]

    def spread(value, used):
        found = {0: value}
        for mask in sorted(range(1, 2 ** len(used)), key=lambda m: (bin(m).count("1"), m)):
            held = [bit for bit in range(len(used)) if mask >> bit & 1]
            chosen = next((bit for bit in held if (bit + 1) % len(used) in held), held[0])
            found[mask] = swapped(found[mask ^ (1 << chosen)], *used[chosen])
        return [found[mask] for mask in range(2 ** len(used))]

    def with_sibling(values):
        return [item for value in values for item in (value, swapped(value, "leaf", 1))]

    other = swapped(leaf_maps, "leaf", 1)
    piece, coupling, bulk = call(
        first_kernel, 2, [(3, half_width, W), (4, width, W), (6, width, W)], [],
        *orders, leaf_maps, other, top_data,
    )
    pieces = with_sibling(across(piece))
    data_other = swapped(top_data, "leaf", 1)
    bulks = spread(bulk, bits)
    inner_rows, inverse_one, coupling_inner, right, right_half = call(
        lambda *refs: second_kernel(count, *refs), 2,
        [(2 * half_width, 2 * W), (W, W), (2 * W, W), (W, 2 * W), (W // 2, 2 * W)], [(W, W)],
        *orders, leaf_maps, other, *pieces,
    )
    summed = inner_rows + swapped(inner_rows, "leaf", 2)
    right_mine = swapped(right_half, "leaf", 2)
    right_other = swapped(right_mine, "leaf", 1)
    (outer_all,) = call(outer_kernel, 2, [(4, width, 2 * W)], [], *orders, leaf_maps, other, coupling, right)
    (inverse_two,) = call(
        lambda *refs: third_kernel(count, *refs), 0, [(2 * W, 2 * W)], [(2 * W, 2 * W)],
        *with_sibling(across(summed)),
    )
    scratch = [(2 * W, W), (2 * W, K), (W, W), (W, W)]
    base, outer_near, driven_near = call(
        lambda *refs: near_kernel(count, *refs), 2,
        [(4, width, 2 * W), (2 * W, 2 * W), (K, 3 * W)], scratch,
        *orders, leaf_maps, other, coupling, inverse_one, right, *bulks[:count],
    )
    outer_far, driven = call(
        lambda *refs: far_kernel(count, *refs), 2, [(2 * W, 2 * W), (K, 3 * W)], scratch + [(W, 2 * W)],
        *orders, driven_near, right_mine, right_other, *bulks[count:],
    )
    driven_other = swapped(driven, "leaf", 1)
    mine, theirs = call(top_kernel, 0, [(2, width, 4 * W)] * 2, [], base, outer_all, inverse_two, outer_near, outer_far)
    received = swapped(theirs, "leaf", 1)
    (leaf_data,) = call(
        leaf_kernel, 2, [(4, width, K)], [(2 * width, K)],
        *orders, top_data, data_other, coupling_inner, inverse_one, inverse_two, driven, driven_other,
    )
    (top_map,) = call(join_kernel, 0, [(2, width, 8 * W)], [], mine, received)
    return (top_map, leaf_data)


def solution(mesh):
    in_specs = (P("leaf", "sub", None), P(), P(), P("leaf", "sub", None))
    out_specs = (P("leaf", "sub", None), P("leaf", "sub", None))

    return jax.shard_map(shards, mesh=mesh, in_specs=in_specs, out_specs=out_specs, check_vma=False)
```

```python
import jax
import jax.numpy as jnp
from jax import lax
from jax.experimental import pallas as pl
from jax.experimental.pallas import tpu as pltpu
from jax.sharding import PartitionSpec as P


W = 256
K = 256
F32 = jnp.float32
BF16 = jnp.bfloat16
NN = (((1,), (0,)), ((), ()))
NT = (((1,), (1,)), ((), ()))

VMEM_MIB = 24


def swapped(value, axis, mask):
    pairs = [(source, source ^ mask) for source in range(lax.axis_size(axis))]
    return lax.ppermute(value, axis, pairs)


def parts_of(value):
    high = value.astype(BF16)
    return high, (value - high.astype(F32)).astype(BF16)


def product(left, right, dims=NN):
    left_high, left_low = left if isinstance(left, tuple) else parts_of(left)
    right_high, right_low = right if isinstance(right, tuple) else parts_of(right)

    def one(a, b):
        return lax.dot_general(a, b, dims, preferred_element_type=F32)

    return one(left_high, right_low) + one(left_low, right_high) + one(left_high, right_high)


def newton(block):
    size = block.shape[0]
    bound = jnp.max(jnp.sum(jnp.abs(block), axis=1, keepdims=True), axis=0, keepdims=True)
    inverse_bound = 1.0 / bound
    rows = lax.broadcasted_iota(jnp.int32, (size, size), 0)
    columns = lax.broadcasted_iota(jnp.int32, (size, size), 1)
    eye = (rows == columns).astype(F32)
    power = eye - block * inverse_bound
    total = (eye + power) * inverse_bound
    split = parts_of(power)
    for _ in range(3):
        power = product(split, split)
        split = parts_of(power)
        total = total + product(total, split)
    return total


class Tree:
    def __init__(self, order_one, order_two):
        self.leaf = lax.axis_index("leaf")
        self.member = lax.axis_index("sub")
        self.half = self.leaf % 2
        self.node = self.leaf // 2
        self.order_one = order_one
        self.order_two = order_two

    def edge(self, position):
        joint = self.order_two[self.node, position]
        which = joint // 3
        return which, self.order_one[joint % 3, 2 * self.node + which]

    def inner(self, which):
        return self.order_one[3, 2 * self.node + which]


def block_of(tree, own, other, which, row_edge, start, size, column_edge):
    column = pl.ds(pl.multiple_of(column_edge * W, W), W)
    rows = pl.ds(start, size)
    return jnp.where(which == tree.half, own[row_edge, rows, column], other[row_edge, rows, column])


def first_kernel(final, order_one, order_two, source, *refs):
    earlier, (piece, coupling, raw) = refs[:-3], refs[-3:]
    if final:
        raw[4:6] = earlier[3][...]
    tree = Tree(order_one, order_two)
    half_width = piece.shape[1]
    width = coupling.shape[1]
    held = tree.half ^ 1 if final else tree.half

    def keep(out, before, slot, which, row_edge, start, size, column_edge):
        column = pl.ds(pl.multiple_of(column_edge * W, W), W)
        value = source[row_edge, pl.ds(start, size), column]
        other = earlier[before][slot] if final else 0.0
        out[slot] = jnp.where(which == held, value, other)

    start = pl.multiple_of(tree.half * half_width, half_width)
    inner = tree.inner(held)
    own_piece = source[inner, pl.ds(start, half_width), pl.ds(pl.multiple_of(inner * W, W), W)]
    piece[0] = own_piece + earlier[0][0] if final else own_piece
    for slot in range(2):
        which, edge = tree.edge(4 + slot)
        keep(piece, 0, 1 + slot, which, edge, start, half_width, tree.inner(which))
    for slot in range(4):
        which, edge = tree.edge(slot)
        keep(coupling, 1, slot, which, edge, 0, width, tree.inner(which))
    same, inner_leaf, outer_leaf = packing(tree, tree.node)
    holder = jnp.where(outer_leaf[0] == inner_leaf[0], 0, 1)
    for slot in range(2):
        raw[slot] = coupling[2 * tree.half + slot]
        row = jnp.where(same, holder, slot)
        column = jnp.where(same, slot, jnp.where(outer_leaf[slot] == inner_leaf[0], 0, 1))
        which, edge = tree.edge(2 * tree.half + row)
        _, column_edge = tree.edge(4 + column)
        keep(raw, 2, 2 + slot, which, edge, 0, width, column_edge)


def packing(tree, node):
    inner_leaf = [tree.order_two[node, 4 + slot] // 3 for slot in range(2)]
    outer_leaf = [tree.order_two[node, 2 * tree.half + slot] // 3 for slot in range(2)]
    return inner_leaf[0] == inner_leaf[1], inner_leaf, outer_leaf


def interface_rows(tree, own, other, position, start, size):
    which, edge = tree.edge(position)
    found = []
    for slot in range(2):
        column_which, column_edge = tree.edge(4 + slot)
        value = block_of(tree, own, other, which, edge, start, size, column_edge)
        found.append(jnp.where(which == column_which, value, 0.0))
    return jnp.concatenate(found, axis=1)


def second_kernel(count, order_one, order_two, own, other, *refs):
    pieces, outs = refs[: 2 * count], refs[2 * count :]
    inner_rows, inverse_out, coupling_inner, right_out, right_half, sums = outs
    tree = Tree(order_one, order_two)
    half_width = pieces[0].shape[1]
    width = 2 * half_width
    for mask in range(count):
        for side in range(2):
            piece = pieces[2 * mask + side]
            row = (tree.member ^ mask) * width + (tree.half ^ side) * half_width
            sums[pl.ds(pl.multiple_of(row, half_width), half_width), :] = piece[0]
            for slot in range(2):
                target = pl.ds(pl.multiple_of(row + slot * W, half_width), half_width)
                coupling_inner[target, :] = piece[1 + slot]
    inverse = newton(sums[...])
    inverse_out[...] = inverse
    right = product(inverse, coupling_inner[...], NT)
    right_out[...] = right
    right_half[...] = right_out[pl.ds(pl.multiple_of(tree.half * (W // 2), W // 2), W // 2), :]
    start = pl.multiple_of(tree.half * half_width, half_width)
    left = jnp.concatenate([pieces[0][1], pieces[0][2]], axis=0)
    change = product(left, right)
    for slot, (row, column) in enumerate(((0, 0), (0, 1), (1, 1))):
        which, edge = tree.edge(4 + row)
        column_which, column_edge = tree.edge(4 + column)
        value = block_of(tree, own, other, which, edge, start, half_width, column_edge)
        value = jnp.where(which == column_which, value, 0.0)
        inner_rows[slot] = value - change[row * half_width : (row + 1) * half_width, column * W : (column + 1) * W]


def outer_kernel(order_one, order_two, own, other, coupling, right, outer_all):
    tree = Tree(order_one, order_two)
    width = coupling.shape[1]
    change = product(coupling[...].reshape(4 * width, W), right[...])
    for slot in range(4):
        base = interface_rows(tree, own, other, slot, 0, width)
        outer_all[slot] = base - change[slot * width : (slot + 1) * width]


def third_kernel(count, *refs):
    pieces, (inverse_out, sums) = refs[: 2 * count], refs[2 * count :]
    half, member = lax.axis_index("leaf") % 2, lax.axis_index("sub")
    half_width = pieces[0].shape[1]
    width = 2 * half_width
    for mask in range(count):
        for side in range(2):
            piece = pieces[2 * mask + side]
            row = pl.multiple_of((member ^ mask) * width + (half ^ side) * half_width, half_width)
            sums[pl.ds(row, half_width), :W] = piece[0]
            sums[pl.ds(row, half_width), W:] = piece[1]
            sums[pl.ds(pl.multiple_of(row + W, half_width), half_width), W:] = piece[2]
    sums[W:, :W] = sums[:W, W:].T
    inverse_out[...] = newton(sums[...])


def gathered(tree, raws, coupling_half, packed_zero, packed_one):
    for mask, (coupling, packed) in enumerate(raws):
        width = coupling.shape[1]
        at = (tree.member ^ mask) * width
        for slot in range(2):
            target = pl.ds(pl.multiple_of(slot * W + at, width), width)
            coupling_half[target, :] = coupling[slot]
        target = pl.ds(pl.multiple_of(at, width), width)
        packed_zero[target, :] = packed[0]
        packed_one[target, :] = packed[1]


def outer_rows(tree, node, coupling_split, packed_zero, packed_one, right, outer_half):
    same, inner_leaf, outer_leaf = packing(tree, node)
    packed = (packed_zero, packed_one)
    change = product(coupling_split, right)
    for slot in range(2):
        rows = slice(slot * W, (slot + 1) * W)
        for column in range(2):
            columns = slice(column * W, (column + 1) * W)
            value = jnp.where(same, packed[column][...], packed[slot][...])
            value = jnp.where(outer_leaf[slot] == inner_leaf[column], value, 0.0)
            outer_half[rows, columns] = value - change[rows, columns]


def near_kernel(count, order_one, order_two, own, other, coupling, inverse_one, right, *refs):
    raws, outs = refs[:count], refs[count:]
    base_out, outer_half, coupling_half, packed_zero, packed_one = outs
    tree = Tree(order_one, order_two)
    width = own.shape[1]
    gathered(tree, [(raw.at[0:2], raw.at[2:4]) for raw in raws], coupling_half, packed_zero, packed_one)
    coupling_split = parts_of(coupling_half[...])
    scaled = product(coupling[...].reshape(4 * width, W), inverse_one[...])
    local = product(scaled, coupling_split, NT)
    for slot in range(4):
        which, edge = tree.edge(slot)
        for column in range(2):
            column_which, column_edge = tree.edge(2 * tree.half + column)
            value = block_of(tree, own, other, which, edge, 0, width, column_edge)
            value = jnp.where(which == column_which, value, 0.0)
            rows, columns = slice(slot * width, (slot + 1) * width), slice(column * W, (column + 1) * W)
            base_out[slot, :, columns] = value - local[rows, columns]
    outer_rows(tree, tree.node, coupling_split, packed_zero, packed_one, right[...], outer_half)


def far_kernel(count, order_one, order_two, outer_near, coupling_near, right_mine, right_other, *refs):
    raws, last, outs = refs[: 2 * count - 1], refs[2 * count - 1 : 2 * count + 2], refs[2 * count + 2 :]
    datas = [raw.at[4:6] for raw in raws] + [last[2]]
    outer_half, driven, coupling_half, packed_zero, packed_one, right, data_half = outs
    tree = Tree(order_one, order_two)
    pairs = [(raw.at[0:2], raw.at[2:4]) for raw in raws[count:]] + [last[:2]]
    gathered(tree, pairs, coupling_half, packed_zero, packed_one)
    for side, held in enumerate((right_mine, right_other)):
        right[pl.ds(pl.multiple_of((tree.half ^ side) * (W // 2), W // 2), W // 2), :] = held[...]
    outer_rows(tree, tree.node ^ 1, parts_of(coupling_half[...]), packed_zero, packed_one, right[...], outer_half)
    for place, data in enumerate(datas):
        width = data.shape[1]
        at = (tree.member ^ (place % count)) * width + (place // count) * 2 * W
        for slot in range(2):
            data_half[pl.ds(pl.multiple_of(slot * W + at, width), width), :] = data[slot]
    near = parts_of(data_half[: 2 * W, :].T)
    far = data_half[2 * W :, :].T
    driven[:, : 2 * W] = product(near, outer_near[...]) + product(far, outer_half[...])
    driven[:, 2 * W :] = product(near, coupling_near[...])


def top_kernel(base, outer_all, inverse_two, outer_near, outer_far, mine, theirs):
    half = lax.axis_index("leaf") % 2
    slots, width, columns = base.shape
    scaled = parts_of(product(outer_all[...].reshape(slots * width, columns), inverse_two[...]))
    for far, outer in enumerate((outer_near, outer_far)):
        part = -product(scaled, outer[...], NT).reshape(slots, width, columns)
        if not far:
            part = base[...] + part
        target = slice(far * columns, (far + 1) * columns)
        mine[:, :, target] = jnp.where(half == 0, part[:2], part[2:])
        theirs[:, :, target] = jnp.where(half == 0, part[2:], part[:2])


def leaf_kernel(order_one, order_two, data_own, data_other, coupling_inner, inverse_one, inverse_two, driven, driven_other, leaf_data, inner):
    tree = Tree(order_one, order_two)
    width = leaf_data.shape[1]
    total = driven[...] + driven_other[...]
    second = parts_of(total[:, : 2 * W])
    lifted = -product(second, inverse_two[...])
    first = total[:, 2 * W :] + product(lifted, coupling_inner[...])
    mine = pl.multiple_of(tree.member * width, width)
    rows = [inverse_two[pl.ds(pl.multiple_of(slot * W + mine, width), width), :] for slot in range(2)]
    inner[...] = -product(jnp.concatenate(rows, axis=0), second, NT)
    leaf_data[order_one[3, tree.leaf]] = -product(inverse_one[pl.ds(mine, width), :], first, NT)
    for slot in range(3):
        joint = 3 * tree.half + slot
        position = 0
        for place in range(6):
            position = position + place * (order_two[tree.node, place] == joint).astype(jnp.int32)
        place = position % 2
        from_data = jnp.where(position // 2 == tree.half, data_own[place], data_other[place])
        from_inner = inner[pl.ds(pl.multiple_of(place * width, width), width), :]
        leaf_data[order_one[slot, tree.leaf]] = jnp.where(position < 4, from_data, from_inner)


def join_kernel(mine, theirs, top_map):
    half, node_bit = lax.axis_index("leaf") % 2, (lax.axis_index("leaf") // 2) % 2
    columns = mine.shape[2] // 2
    for far in range(2):
        source = slice(far * columns, (far + 1) * columns)
        for side, held in enumerate((mine, theirs)):
            target = pl.multiple_of((2 * (node_bit ^ far) + (half ^ side)) * columns, columns)
            top_map[:, :, pl.ds(target, columns)] = held[:, :, source]


def call(kernel, scalar_count, outs, scratch, *args):
    smem = pl.BlockSpec(memory_space=pltpu.SMEM)
    vmem = pl.BlockSpec(memory_space=pltpu.VMEM)
    return pl.pallas_call(
        kernel,
        in_specs=[smem] * scalar_count + [vmem] * (len(args) - scalar_count),
        out_specs=[vmem] * len(outs),
        out_shape=[jax.ShapeDtypeStruct(shape, F32) for shape in outs],
        scratch_shapes=[pltpu.VMEM(shape, F32) for shape in scratch],
        compiler_params=pltpu.CompilerParams(vmem_limit_bytes=VMEM_MIB * 2**20),
    )(*args)


def shards(leaf_maps, order_one, order_two, top_data):
    width = leaf_maps.shape[1]
    half_width = width // 2
    count = lax.axis_size("sub")
    bits = [("sub", 2**bit) for bit in range((count - 1).bit_length())] + [("leaf", 2)]
    orders = (order_one.T, order_two)

    def across(value):
        found = {0: value}
        for mask in sorted(range(1, count), key=lambda m: (-bin(m).count("1"), m)):
            found[mask] = swapped(value, "sub", mask)
        return [found[mask] for mask in range(count)]

    def spread(value, last):
        found = {0: value}
        for mask in sorted(range(1, 2 * count - 1), key=lambda m: (bin(m).count("1"), m)):
            held = [bit for bit in range(len(bits)) if mask >> bit & 1]
            chosen = next((bit for bit in held if (bit + 1) % len(bits) in held), held[0])
            found[mask] = swapped(found[mask ^ (1 << chosen)], *bits[chosen])
        top = 2 * count - 1
        found[top] = []
        for first, end, chosen in last:
            found[top].append(swapped(found[top ^ (1 << chosen)][first:end], *bits[chosen]))
        return [found[mask] for mask in range(2 * count)]

    def with_sibling(values):
        found = []
        for value in values:
            found += [value, swapped(value, "leaf", 1)]
        return found

    other = swapped(leaf_maps, "leaf", 1)
    first_outs = [(3, half_width, W), (4, width, W)]
    early = call(lambda *refs: first_kernel(False, *refs), 2, first_outs + [(4, width, W)], [], *orders, leaf_maps)
    piece, coupling, raw = call(
        lambda *refs: first_kernel(True, *refs), 2, first_outs + [(6, width, W)], [], *orders, other, *early, top_data
    )
    own = leaf_maps
    pieces = with_sibling(across(piece))
    data_other = swapped(top_data, "leaf", 1)
    raws = spread(raw, [(2 * part, 2 * part + 2, part % len(bits)) for part in range(3)])
    inner_rows, inverse_one, coupling_inner, right, right_half = call(
        lambda *refs: second_kernel(count, *refs), 2,
        [(3, half_width, W), (W, W), (2 * W, W), (W, 2 * W), (W // 2, 2 * W)], [(W, W)],
        *orders, own, other, *pieces,
    )
    summed = inner_rows + swapped(inner_rows, "leaf", 2)
    right_mine = swapped(right_half, "leaf", 2)
    right_other = swapped(right_mine, "leaf", 1)
    (outer_all,) = call(outer_kernel, 2, [(4, width, 2 * W)], [], *orders, own, other, coupling, right)
    (inverse_two,) = call(
        lambda *refs: third_kernel(count, *refs), 0, [(2 * W, 2 * W)], [(2 * W, 2 * W)],
        *with_sibling(across(summed)),
    )
    base, outer_near, coupling_near = call(
        lambda *refs: near_kernel(count, *refs), 2,
        [(4, width, 2 * W), (2 * W, 2 * W), (2 * W, W)], [(W, W), (W, W)],
        *orders, own, other, coupling, inverse_one, right, *raws[:count],
    )
    outer_far, driven = call(
        lambda *refs: far_kernel(count, *refs), 2, [(2 * W, 2 * W), (K, 3 * W)],
        [(2 * W, W), (W, W), (W, W), (W, 2 * W), (4 * W, K)],
        *orders, outer_near, coupling_near, right_mine, right_other,
        *raws[:-1], *raws[-1],
    )
    driven_other = swapped(driven, "leaf", 1)
    mine, theirs = call(top_kernel, 0, [(2, width, 4 * W)] * 2, [], base, outer_all, inverse_two, outer_near, outer_far)
    received = swapped(theirs, "leaf", 1)
    (leaf_data,) = call(
        leaf_kernel, 2, [(4, width, K)], [(2 * width, K)],
        *orders, top_data, data_other, coupling_inner, inverse_one, inverse_two, driven, driven_other,
    )
    (top_map,) = call(join_kernel, 0, [(2, width, 8 * W)], [], mine, received)
    return (top_map, leaf_data)


def solution(mesh):
    in_specs = (P("leaf", "sub", None), P(), P(), P("leaf", "sub", None))
    out_specs = (P("leaf", "sub", None), P("leaf", "sub", None))

    return jax.shard_map(shards, mesh=mesh, in_specs=in_specs, out_specs=out_specs, check_vma=False)
```

```python
import jax
import jax.numpy as jnp
from jax import lax
from jax.experimental import pallas as pl
from jax.experimental.pallas import tpu as pltpu
from jax.sharding import PartitionSpec as P


W = 256
K = 256
F32 = jnp.float32
BF16 = jnp.bfloat16
NN = (((1,), (0,)), ((), ()))
NT = (((1,), (1,)), ((), ()))

VMEM_MIB = 24


def swapped(value, axis, mask):
    pairs = [(source, source ^ mask) for source in range(lax.axis_size(axis))]
    return lax.ppermute(value, axis, pairs)


def parts_of(value):
    high = value.astype(BF16)
    return high, (value - high.astype(F32)).astype(BF16)


def product(left, right, dims=NN):
    left_high, left_low = left if isinstance(left, tuple) else parts_of(left)
    right_high, right_low = right if isinstance(right, tuple) else parts_of(right)

    def one(a, b):
        return lax.dot_general(a, b, dims, preferred_element_type=F32)

    if left_high.shape[0] <= W // 2 or left_high.shape == right_high.shape == (W, W):
        (left_axis,), (right_axis,) = dims[0]
        lefts = jnp.concatenate([left_high, left_low, left_high], axis=left_axis)
        return one(lefts, jnp.concatenate([right_low, right_high, right_high], axis=right_axis))
    return one(left_high, right_low) + one(left_low, right_high) + one(left_high, right_high)


def newton(block):
    size = block.shape[0]
    bound = jnp.max(jnp.sum(jnp.abs(block), axis=1, keepdims=True), axis=0, keepdims=True)
    inverse_bound = 1.0 / bound
    rows = lax.broadcasted_iota(jnp.int32, (size, size), 0)
    columns = lax.broadcasted_iota(jnp.int32, (size, size), 1)
    eye = (rows == columns).astype(F32)
    power = eye - block * inverse_bound
    total = (eye + power) * inverse_bound
    split = parts_of(power)
    for _ in range(3):
        power = product(split, split)
        split = parts_of(power)
        total = total + product(total, split)
    return total


class Tree:
    def __init__(self, order_one, order_two):
        self.leaf = lax.axis_index("leaf")
        self.member = lax.axis_index("sub")
        self.half = self.leaf % 2
        self.node = self.leaf // 2
        self.order_one = order_one
        self.order_two = order_two

    def edge(self, position):
        joint = self.order_two[self.node, position]
        which = joint // 3
        return which, self.order_one[joint % 3, 2 * self.node + which]

    def inner(self, which):
        return self.order_one[3, 2 * self.node + which]


def block_of(tree, own, other, which, row_edge, start, size, column_edge):
    column = pl.ds(pl.multiple_of(column_edge * W, W), W)
    rows = pl.ds(start, size)
    return jnp.where(which == tree.half, own[row_edge, rows, column], other[row_edge, rows, column])


def first_kernel(final, order_one, order_two, source, *refs):
    earlier, (piece, coupling, raw) = refs[:-3], refs[-3:]
    if final:
        raw[4:6] = earlier[3][...]
    tree = Tree(order_one, order_two)
    half_width = piece.shape[1]
    width = coupling.shape[1]
    held = tree.half ^ 1 if final else tree.half

    def keep(out, before, slot, which, row_edge, start, size, column_edge):
        column = pl.ds(pl.multiple_of(column_edge * W, W), W)
        value = source[row_edge, pl.ds(start, size), column]
        other = earlier[before][slot] if final else 0.0
        out[slot] = jnp.where(which == held, value, other)

    start = pl.multiple_of(tree.half * half_width, half_width)
    inner = tree.inner(held)
    own_piece = source[inner, pl.ds(start, half_width), pl.ds(pl.multiple_of(inner * W, W), W)]
    piece[0] = own_piece + earlier[0][0] if final else own_piece
    for slot in range(2):
        which, edge = tree.edge(4 + slot)
        keep(piece, 0, 1 + slot, which, edge, start, half_width, tree.inner(which))
    for slot in range(4):
        which, edge = tree.edge(slot)
        keep(coupling, 1, slot, which, edge, 0, width, tree.inner(which))
    same, inner_leaf, outer_leaf = packing(tree, tree.node)
    holder = jnp.where(outer_leaf[0] == inner_leaf[0], 0, 1)
    for slot in range(2):
        raw[slot] = coupling[2 * tree.half + slot]
        row = jnp.where(same, holder, slot)
        column = jnp.where(same, slot, jnp.where(outer_leaf[slot] == inner_leaf[0], 0, 1))
        which, edge = tree.edge(2 * tree.half + row)
        _, column_edge = tree.edge(4 + column)
        keep(raw, 2, 2 + slot, which, edge, 0, width, column_edge)


def packing(tree, node):
    inner_leaf = [tree.order_two[node, 4 + slot] // 3 for slot in range(2)]
    outer_leaf = [tree.order_two[node, 2 * tree.half + slot] // 3 for slot in range(2)]
    return inner_leaf[0] == inner_leaf[1], inner_leaf, outer_leaf


def interface_rows(tree, own, other, position, start, size):
    which, edge = tree.edge(position)
    found = []
    for slot in range(2):
        column_which, column_edge = tree.edge(4 + slot)
        value = block_of(tree, own, other, which, edge, start, size, column_edge)
        found.append(jnp.where(which == column_which, value, 0.0))
    return jnp.concatenate(found, axis=1)


def second_kernel(count, order_one, order_two, own, other, *refs):
    pieces, outs = refs[: 2 * count], refs[2 * count :]
    inner_rows, inverse_out, coupling_inner, sums = outs
    tree = Tree(order_one, order_two)
    half_width = pieces[0].shape[1]
    width = 2 * half_width
    for mask in range(count):
        for side in range(2):
            piece = pieces[2 * mask + side]
            row = (tree.member ^ mask) * width + (tree.half ^ side) * half_width
            sums[pl.ds(pl.multiple_of(row, half_width), half_width), :] = piece[0]
            for slot in range(2):
                target = pl.ds(pl.multiple_of(row + slot * W, half_width), half_width)
                coupling_inner[target, :] = piece[1 + slot]
    inverse = newton(sums[...])
    inverse_out[...] = inverse
    start = pl.multiple_of(tree.half * half_width, half_width)
    left = jnp.concatenate([pieces[0][1], pieces[0][2]], axis=0)
    change = product(product(left, inverse), coupling_inner[...], NT)
    for slot, (row, column) in enumerate(((0, 0), (0, 1), (1, 1))):
        which, edge = tree.edge(4 + row)
        column_which, column_edge = tree.edge(4 + column)
        value = block_of(tree, own, other, which, edge, start, half_width, column_edge)
        value = jnp.where(which == column_which, value, 0.0)
        inner_rows[slot] = value - change[row * half_width : (row + 1) * half_width, column * W : (column + 1) * W]


def outer_kernel(order_one, order_two, own, other, coupling, inverse_one, coupling_inner, outer_all, right_out, right_half):
    tree = Tree(order_one, order_two)
    width = coupling.shape[1]
    right = product(inverse_one[...], coupling_inner[...], NT)
    right_out[...] = right
    right_half[...] = right_out[pl.ds(pl.multiple_of(tree.half * (W // 2), W // 2), W // 2), :]
    change = product(coupling[...].reshape(4 * width, W), right)
    for slot in range(4):
        base = interface_rows(tree, own, other, slot, 0, width)
        outer_all[slot] = base - change[slot * width : (slot + 1) * width]


def third_kernel(count, *refs):
    pieces, (inverse_out, sums) = refs[: 2 * count], refs[2 * count :]
    half, member = lax.axis_index("leaf") % 2, lax.axis_index("sub")
    half_width = pieces[0].shape[1]
    width = 2 * half_width
    for mask in range(count):
        for side in range(2):
            piece = pieces[2 * mask + side]
            row = pl.multiple_of((member ^ mask) * width + (half ^ side) * half_width, half_width)
            sums[pl.ds(row, half_width), :W] = piece[0]
            sums[pl.ds(row, half_width), W:] = piece[1]
            sums[pl.ds(pl.multiple_of(row + W, half_width), half_width), W:] = piece[2]
    sums[W:, :W] = sums[:W, W:].T
    inverse_out[...] = newton(sums[...])


def gathered(tree, raws, coupling_half, packed_zero, packed_one):
    for mask, (coupling, packed) in enumerate(raws):
        width = coupling.shape[1]
        at = (tree.member ^ mask) * width
        for slot in range(2):
            target = pl.ds(pl.multiple_of(slot * W + at, width), width)
            coupling_half[target, :] = coupling[slot]
        target = pl.ds(pl.multiple_of(at, width), width)
        packed_zero[target, :] = packed[0]
        packed_one[target, :] = packed[1]


def outer_rows(tree, node, coupling_split, packed_zero, packed_one, right, outer_half):
    same, inner_leaf, outer_leaf = packing(tree, node)
    packed = (packed_zero, packed_one)
    change = product(coupling_split, right)
    for slot in range(2):
        rows = slice(slot * W, (slot + 1) * W)
        for column in range(2):
            columns = slice(column * W, (column + 1) * W)
            value = jnp.where(same, packed[column][...], packed[slot][...])
            value = jnp.where(outer_leaf[slot] == inner_leaf[column], value, 0.0)
            outer_half[rows, columns] = value - change[rows, columns]


def driven_by(tree, raws, data_half):
    for mask, raw in enumerate(raws):
        width = raw.shape[1]
        at = (tree.member ^ mask) * width
        for slot in range(2):
            data_half[pl.ds(pl.multiple_of(slot * W + at, width), width), :] = raw[slot]
    return parts_of(data_half[...].T)


def share(tree, part, mine, theirs):
    mine[...] = jnp.where(tree.half == 0, part[:2], part[2:])
    theirs[...] = jnp.where(tree.half == 0, part[2:], part[:2])


def near_kernel(count, order_one, order_two, own, other, coupling, inverse_one, right, outer_all, inverse_two, *refs):
    raws, outs = refs[:count], refs[count:]
    mine, theirs, scaled_out, driven, coupling_half, packed_zero, packed_one, outer_half, data_half, part = outs
    tree = Tree(order_one, order_two)
    width = own.shape[1]
    gathered(tree, [(raw.at[0:2], raw.at[2:4]) for raw in raws], coupling_half, packed_zero, packed_one)
    coupling_split = parts_of(coupling_half[...])
    outer_rows(tree, tree.node, coupling_split, packed_zero, packed_one, right[...], outer_half)
    outer_split = parts_of(outer_half[...])
    scaled_out[...] = product(outer_all[...].reshape(4 * width, 2 * W), inverse_two[...])
    scaled = product(coupling[...].reshape(4 * width, W), inverse_one[...])
    change = product(scaled, coupling_split, NT) + product(scaled_out[...], outer_split, NT)
    for slot in range(4):
        which, edge = tree.edge(slot)
        for column in range(2):
            column_which, column_edge = tree.edge(2 * tree.half + column)
            value = block_of(tree, own, other, which, edge, 0, width, column_edge)
            value = jnp.where(which == column_which, value, 0.0)
            rows, columns = slice(slot * width, (slot + 1) * width), slice(column * W, (column + 1) * W)
            part[slot, :, columns] = value - change[rows, columns]
    share(tree, part, mine, theirs)
    turned = driven_by(tree, [raw.at[4:6] for raw in raws], data_half)
    driven[:, : 2 * W] = product(turned, outer_split)
    driven[:, 2 * W :] = product(turned, coupling_split)


def far_kernel(count, order_one, order_two, driven_near, right_mine, right_other, *refs):
    raws, last, outs = refs[: count - 1], refs[count - 1 : count + 2], refs[count + 2 :]
    outer_half, driven, coupling_half, packed_zero, packed_one, right, data_half = outs
    tree = Tree(order_one, order_two)
    pairs = [(raw.at[0:2], raw.at[2:4]) for raw in raws] + [last[:2]]
    gathered(tree, pairs, coupling_half, packed_zero, packed_one)
    for side, held in enumerate((right_mine, right_other)):
        right[pl.ds(pl.multiple_of((tree.half ^ side) * (W // 2), W // 2), W // 2), :] = held[...]
    outer_rows(tree, tree.node ^ 1, parts_of(coupling_half[...]), packed_zero, packed_one, right[...], outer_half)
    turned = driven_by(tree, [raw.at[4:6] for raw in raws] + [last[2]], data_half)
    driven[:, : 2 * W] = driven_near[:, : 2 * W] + product(turned, outer_half[...])
    driven[:, 2 * W :] = driven_near[:, 2 * W :]


def top_kernel(order_one, order_two, scaled, outer_far, mine, theirs):
    tree = Tree(order_one, order_two)
    part = -product(scaled[...], outer_far[...], NT)
    share(tree, part.reshape(2 * mine.shape[0], mine.shape[1], mine.shape[2]), mine, theirs)


def leaf_kernel(order_one, order_two, data_own, data_other, coupling_inner, inverse_one, inverse_two, driven, driven_other, leaf_data, inner):
    tree = Tree(order_one, order_two)
    width = leaf_data.shape[1]
    total = driven[...] + driven_other[...]
    second = parts_of(total[:, : 2 * W])
    lifted = -product(second, inverse_two[...])
    first = total[:, 2 * W :] + product(lifted, coupling_inner[...])
    mine = pl.multiple_of(tree.member * width, width)
    rows = [inverse_two[pl.ds(pl.multiple_of(slot * W + mine, width), width), :] for slot in range(2)]
    inner[...] = -product(jnp.concatenate(rows, axis=0), second, NT)
    leaf_data[order_one[3, tree.leaf]] = -product(inverse_one[pl.ds(mine, width), :], first, NT)
    for slot in range(3):
        joint = 3 * tree.half + slot
        position = 0
        for place in range(6):
            position = position + place * (order_two[tree.node, place] == joint).astype(jnp.int32)
        place = position % 2
        from_data = jnp.where(position // 2 == tree.half, data_own[place], data_other[place])
        from_inner = inner[pl.ds(pl.multiple_of(place * width, width), width), :]
        leaf_data[order_one[slot, tree.leaf]] = jnp.where(position < 4, from_data, from_inner)


def join_kernel(mine_near, theirs_near, mine_far, theirs_far, top_map):
    half, node_bit = lax.axis_index("leaf") % 2, (lax.axis_index("leaf") // 2) % 2
    columns = mine_near.shape[2]
    for far, pair in enumerate(((mine_near, theirs_near), (mine_far, theirs_far))):
        for side, held in enumerate(pair):
            target = pl.multiple_of((2 * (node_bit ^ far) + (half ^ side)) * columns, columns)
            top_map[:, :, pl.ds(target, columns)] = held[...]


def call(kernel, scalar_count, outs, scratch, *args):
    smem = pl.BlockSpec(memory_space=pltpu.SMEM)
    vmem = pl.BlockSpec(memory_space=pltpu.VMEM)
    return pl.pallas_call(
        kernel,
        in_specs=[smem] * scalar_count + [vmem] * (len(args) - scalar_count),
        out_specs=[vmem] * len(outs),
        out_shape=[jax.ShapeDtypeStruct(shape, F32) for shape in outs],
        scratch_shapes=[pltpu.VMEM(shape, F32) for shape in scratch],
        compiler_params=pltpu.CompilerParams(vmem_limit_bytes=VMEM_MIB * 2**20),
    )(*args)


def shards(leaf_maps, order_one, order_two, top_data):
    width = leaf_maps.shape[1]
    half_width = width // 2
    count = lax.axis_size("sub")
    bits = [("sub", 2**bit) for bit in range((count - 1).bit_length())] + [("leaf", 2)]
    orders = (order_one.T, order_two)

    def across(value):
        found = {0: value}
        for mask in sorted(range(1, count), key=lambda m: (-bin(m).count("1"), m)):
            found[mask] = swapped(value, "sub", mask)
        return [found[mask] for mask in range(count)]

    def spread(value, last):
        found = {0: value}
        for mask in sorted(range(1, 2 * count - 1), key=lambda m: (bin(m).count("1"), m)):
            held = [bit for bit in range(len(bits)) if mask >> bit & 1]
            chosen = next((bit for bit in held if (bit + 1) % len(bits) in held), held[0])
            found[mask] = swapped(found[mask ^ (1 << chosen)], *bits[chosen])
        top = 2 * count - 1
        found[top] = []
        for first, end, chosen in last:
            found[top].append(swapped(found[top ^ (1 << chosen)][first:end], *bits[chosen]))
        return [found[mask] for mask in range(2 * count)]

    def with_sibling(values):
        found = []
        for value in values:
            found += [value, swapped(value, "leaf", 1)]
        return found

    other = swapped(leaf_maps, "leaf", 1)
    first_outs = [(3, half_width, W), (4, width, W)]
    early = call(lambda *refs: first_kernel(False, *refs), 2, first_outs + [(4, width, W)], [], *orders, leaf_maps)
    piece, coupling, raw = call(
        lambda *refs: first_kernel(True, *refs), 2, first_outs + [(6, width, W)], [], *orders, other, *early, top_data
    )
    own = leaf_maps
    pieces = with_sibling(across(piece))
    data_other = swapped(top_data, "leaf", 1)
    raws = spread(raw, [(2 * part, 2 * part + 2, part % len(bits)) for part in range(3)])
    inner_rows, inverse_one, coupling_inner = call(
        lambda *refs: second_kernel(count, *refs), 2,
        [(3, half_width, W), (W, W), (2 * W, W)], [(W, W)],
        *orders, own, other, *pieces,
    )
    summed = inner_rows + swapped(inner_rows, "leaf", 2)
    outer_all, right, right_half = call(
        outer_kernel, 2, [(4, width, 2 * W), (W, 2 * W), (W // 2, 2 * W)], [],
        *orders, own, other, coupling, inverse_one, coupling_inner,
    )
    right_mine = swapped(right_half, "leaf", 2)
    right_other = swapped(right_mine, "leaf", 1)
    (inverse_two,) = call(
        lambda *refs: third_kernel(count, *refs), 0, [(2 * W, 2 * W)], [(2 * W, 2 * W)],
        *with_sibling(across(summed)),
    )
    halves = [(2, width, 2 * W)] * 2
    scratch = [(2 * W, W), (W, W), (W, W)]
    mine_near, theirs_near, scaled, driven_near = call(
        lambda *refs: near_kernel(count, *refs), 2,
        halves + [(4 * width, 2 * W), (K, 3 * W)], scratch + [(2 * W, 2 * W), (2 * W, K), (4, width, 2 * W)],
        *orders, own, other, coupling, inverse_one, right, outer_all, inverse_two, *raws[:count],
    )
    received_near = swapped(theirs_near, "leaf", 1)
    outer_far, driven = call(
        lambda *refs: far_kernel(count, *refs), 2, [(2 * W, 2 * W), (K, 3 * W)],
        scratch + [(W, 2 * W), (2 * W, K)],
        *orders, driven_near, right_mine, right_other, *raws[count:-1], *raws[-1],
    )
    driven_other = swapped(driven, "leaf", 1)
    mine_far, theirs_far = call(top_kernel, 2, halves, [], *orders, scaled, outer_far)
    received_far = swapped(theirs_far, "leaf", 1)
    (leaf_data,) = call(
        leaf_kernel, 2, [(4, width, K)], [(2 * width, K)],
        *orders, top_data, data_other, coupling_inner, inverse_one, inverse_two, driven, driven_other,
    )
    (top_map,) = call(join_kernel, 0, [(2, width, 8 * W)], [], mine_near, received_near, mine_far, received_far)
    return (top_map, leaf_data)


def solution(mesh):
    in_specs = (P("leaf", "sub", None), P(), P(), P("leaf", "sub", None))
    out_specs = (P("leaf", "sub", None), P("leaf", "sub", None))

    return jax.shard_map(shards, mesh=mesh, in_specs=in_specs, out_specs=out_specs, check_vma=False)
```
